256 devices in a mesh: cube: 32 (over y, x, core), grid: 8 (over z).
Axes of the slice: x: 4, y: 4, z: 8, core: 2. Of those that a mesh axis runs over, the one named last changes fastest.
Arguments:
- child_update: bfloat16 [8192, 16384], P('cube', 'grid'), may hold values from -6 to 6
- child_panel: bfloat16 [512, 8192], P('grid', 'cube'), may hold values from -6 to 6
- panel_entries: bfloat16 [512, 32768], P('grid', 'cube'), may hold values from -6 to 6
- panel_inverse: bfloat16 [512, 512], replicated, as said below
- block_owner: int32 [1024], replicated, may hold values from 0 to 31, as said below
- child_dest: int32 [512], replicated, may hold values from 0 to 1023, as said below
- child_rows: int32 [512, 16], P('cube'), may hold values from 0 to 15, each once within a row
Outputs:
- schur_update: bfloat16 [32768, 16384], P('cube', 'grid')
- panel_factor: bfloat16 [512, 32768], P('grid', 'cube')
The draws below stay inside these ranges and needn't reach their ends.
Inputs may be any that keep to these rules, and one draw needn't show every extreme that they name: `block_owner`: row blocks r*128 to (r+1)*128 - 1 form column range r. One cube index owns at most 8 row blocks of one range, and in every draw some cube index owns exactly 8 of some range. Every cube index owns at least one row block. `child_dest`: entry s*16+k names the parent row block into which child row block k of cube index s adds. The 16 child row blocks of one cube index go to blocks of 16 different owners, and in every draw some owner receives a block from every cube index. `panel_inverse`: zero below the diagonal, positive on it.
All inputs are finite; a program needn't handle non-finite values.
Results may differ from the reference program's by a relative error of at most 0.0057.
Values may be sent and summed in bfloat16 or wider, within the bound.
A program may use at most 64 MiB of HBM per device.

```python
import math
import jax
import jax.numpy as jnp
from jax import lax

PANEL = 512
BLOCK = 16
RANGE_MEAN = 4
RANGE_CAP = 8
SLOTS = 64
RANGE_BLOCKS = 128
UPDATE = 16384
CHILD_DEV = 16
CHILD_ROWS = 8192
SLOT_ROWS = 32768
N_CUBE = 32
N_GRID = 8


def owner_table(key):
    owner_key = jax.random.fold_in(key, 101)
    perm_key, pair_key, order_key = jax.random.split(owner_key, 3)
    pair_count = N_CUBE // 2
    orders = jax.vmap(lambda subkey: jax.random.permutation(subkey, N_CUBE))(jax.random.split(perm_key, N_GRID))
    shifts = jax.random.randint(pair_key, (N_GRID, pair_count), 0, RANGE_MEAN + 1)
    first_range = jnp.arange(N_GRID, dtype=jnp.int32)[:, None] == 0
    shifts = jnp.where(first_range, jnp.minimum(shifts, RANGE_MEAN - 1), shifts)
    leading_pair = jnp.arange(pair_count, dtype=jnp.int32)[None, :] == 0
    shifts = jnp.where(leading_pair & jnp.logical_not(first_range), RANGE_MEAN, shifts)
    values = jnp.concatenate([RANGE_MEAN + shifts, RANGE_MEAN - shifts], axis=1).astype(jnp.int32)
    range_rows = jnp.broadcast_to(jnp.arange(N_GRID, dtype=jnp.int32)[:, None], (N_GRID, N_CUBE))
    counts = jnp.zeros((N_GRID, N_CUBE), jnp.int32).at[range_rows, orders].set(values)
    bounds = jnp.cumsum(counts, axis=1)
    position = jnp.arange(RANGE_BLOCKS, dtype=jnp.int32)
    sorted_owner = jnp.sum((bounds[:, None, :] <= position[None, :, None]).astype(jnp.int32), axis=2)
    shuffled = jax.vmap(lambda subkey, entries: jax.random.permutation(subkey, entries))(jax.random.split(order_key, N_GRID), sorted_owner)
    return shuffled.reshape(-1).astype(jnp.int32)


def draw_block_owner(key, part):
    return owner_table(key)


def draw_child_dest(key, part):
    owners = owner_table(key)
    hub_key, perm_key, pick_key = jax.random.split(jax.random.fold_in(key, 202), 3)
    hub_owner = jax.random.randint(hub_key, (), 0, N_CUBE)
    orders = jax.vmap(lambda subkey: jax.random.permutation(subkey, N_CUBE))(jax.random.split(perm_key, N_CUBE))
    chosen = orders[:, :CHILD_DEV]
    present = jnp.any(chosen == hub_owner, axis=1)
    leading = jnp.where(present, chosen[:, 0], hub_owner)
    chosen = jnp.concatenate([leading[:, None], chosen[:, 1:]], axis=1).reshape(-1)
    member = (owners[None, :] == chosen[:, None]).astype(jnp.int32)
    totals = jnp.sum(member, axis=1)
    picks = jax.random.randint(pick_key, chosen.shape, 0, 1048576) % totals
    running = jnp.cumsum(member, axis=1)
    return jnp.sum((running <= picks[:, None]).astype(jnp.int32), axis=1).astype(jnp.int32)


def draw_panel_inverse(key, part):
    off_key, diag_key = jax.random.split(jax.random.fold_in(key, 303))
    row_ids = jnp.arange(PANEL, dtype=jnp.int32)[:, None]
    col_ids = jnp.arange(PANEL, dtype=jnp.int32)[None, :]
    spread = jax.random.normal(off_key, (PANEL, PANEL), jnp.float32)
    spread = spread * (0.19 / math.sqrt(PANEL))
    diagonal = jnp.exp(jax.random.uniform(diag_key, (PANEL,), jnp.float32, math.log(0.05), math.log(0.2)))
    upper = jnp.where(col_ids > row_ids, spread, 0.0)
    whole = jnp.where(col_ids == row_ids, diagonal[None, :], upper)
    return whole.astype(jnp.bfloat16)


def block_scale(key, dims, pieces, smallest, largest):
    gain, own = 1.0, jax.random.fold_in(key, 6)
    for dim, shards_of in pieces:
        steps = jnp.exp(jax.random.uniform(jax.random.fold_in(own, dim), (shards_of,), jnp.float32, smallest / len(pieces), largest / len(pieces)))
        gain = gain * jnp.repeat(steps, dims[dim] // shards_of).reshape([-1 if axis == dim else 1 for axis in range(len(dims))])
    return gain


def normal_values(key, dims, width, limit, pieces=(), kind=jnp.bfloat16):
    factor_of = block_scale(key, dims, pieces, -0.22, 0.18) if pieces else 1.0
    result = jax.random.normal(key, dims, jnp.float32) * width * factor_of
    return jnp.minimum(jnp.maximum(result, -limit), limit).astype(kind)


def setup_inputs(seed: int = 0) -> dict:
    streams_of = jax.random.split(jax.random.key(seed), 8)
    child_update = normal_values(streams_of[0], (CHILD_ROWS, UPDATE), 1.0, 6.0, ((0, 32), (1, 8)))
    child_panel = normal_values(streams_of[1], (PANEL, CHILD_ROWS), 1.0, 6.0, ((0, 8), (1, 32)))
    panel_entries = normal_values(streams_of[2], (PANEL, SLOT_ROWS), 1.0, 6.0, ((0, 8), (1, 32)))
    panel_inverse = draw_panel_inverse(jax.random.fold_in(streams_of[7], 71), 0)
    block_owner = draw_block_owner(jax.random.fold_in(streams_of[7], 71), 0)
    child_dest = draw_child_dest(jax.random.fold_in(streams_of[7], 71), 0)
    child_rows = jax.vmap(lambda own: jax.random.permutation(own, BLOCK))(jax.random.split(streams_of[6], (N_CUBE * CHILD_DEV))).reshape((N_CUBE * CHILD_DEV, BLOCK)).astype(jnp.int32)
    return {"child_update": child_update, "child_panel": child_panel, "panel_entries": panel_entries, "panel_inverse": panel_inverse, "block_owner": block_owner, "child_dest": child_dest, "child_rows": child_rows}


def slot_of_blocks(block_owner):
    grouped = block_owner.reshape(N_GRID, RANGE_BLOCKS)
    owner_ids = jnp.arange(N_CUBE, dtype=jnp.int32)
    onehot = (grouped[:, :, None] == owner_ids[None, None, :]).astype(jnp.int32)
    running = jnp.cumsum(onehot, axis=1)
    block_rank = jnp.sum(onehot * running, axis=2) - 1
    range_ids = jnp.arange(N_GRID, dtype=jnp.int32)[:, None]
    return (grouped * SLOTS + range_ids * RANGE_CAP + block_rank).reshape(-1)


def reference(child_update, child_panel, panel_entries, panel_inverse, block_owner, child_dest, child_rows):
    within = jnp.arange(BLOCK, dtype=jnp.int32)
    slot_rows = (slot_of_blocks(block_owner)[:, None] * BLOCK + within[None, :]).reshape(-1)
    target = (child_dest[:, None] * BLOCK + child_rows).reshape(-1)
    front_update = jnp.zeros((UPDATE, UPDATE), jnp.float32).at[target].add(child_update.astype(jnp.float32))
    own_panel = jnp.take(panel_entries, slot_rows, axis=1).astype(jnp.float32)
    child_sum = jnp.zeros((PANEL, UPDATE), jnp.float32).at[:, target].add(child_panel.astype(jnp.float32))
    front_panel = (own_panel + child_sum).astype(jnp.bfloat16)
    factor = jnp.dot(panel_inverse.T, front_panel, preferred_element_type=jnp.float32).astype(jnp.bfloat16)
    row_step = math.gcd(UPDATE, 1024)

    def update_rows(first_row):
        factor_rows = lax.dynamic_slice_in_dim(factor, first_row, row_step, 1)
        front_rows = lax.dynamic_slice_in_dim(front_update, first_row, row_step, 0)
        product = jnp.dot(factor_rows.T, factor, preferred_element_type=jnp.float32)
        return (front_rows - product).astype(jnp.bfloat16)

    starts = jnp.arange(UPDATE // row_step, dtype=jnp.int32) * row_step
    schur = lax.map(update_rows, starts).reshape(UPDATE, UPDATE)
    schur_update = jnp.zeros((SLOT_ROWS, UPDATE), jnp.bfloat16).at[slot_rows].set(schur)
    panel_factor = jnp.zeros((PANEL, SLOT_ROWS), jnp.bfloat16).at[:, slot_rows].set(factor)
    return schur_update, panel_factor
```

```python
import functools

import jax
import jax.numpy as jnp
from jax import lax
from jax.experimental import pallas as pl
from jax.experimental.pallas import tpu as pltpu
from jax.sharding import PartitionSpec as P

MESH = pl.DeviceIdType.MESH
BLOCK = 16
PIECE = 128
EARLY = 16


def iota(shape, dim):
    return lax.broadcasted_iota(jnp.int32, shape, dim)


def onehot(cond, dtype=jnp.bfloat16):
    return jnp.where(cond, 1.0, 0.0).astype(dtype)


def dot(lhs, rhs):
    return jnp.dot(lhs, rhs, preferred_element_type=jnp.float32)


def dot_nt(lhs, rhs):
    return lax.dot_general(lhs, rhs, (((1,), (1,)), ((), ())), preferred_element_type=jnp.float32)


def index_tables(cube, owner_ref, dest_ref, rows_ref):
    owners = owner_ref[...]
    hot = jnp.concatenate(
        [onehot(iota((32, 128), 0) == owners[r : r + 1, :], jnp.float32) for r in range(8)], axis=0
    )
    before = onehot(iota((128, 128), 0) < iota((128, 128), 1))
    running = dot(hot.astype(jnp.bfloat16), before)
    picked = hot * running
    rank = jnp.concatenate(
        [jnp.sum(picked[32 * r : 32 * r + 32], axis=0, keepdims=True) for r in range(8)], axis=0
    )
    owners_f = owners.astype(jnp.float32)
    slot = rank + 8.0 * iota((8, 128), 0).astype(jnp.float32)
    table = jnp.concatenate([owners_f, slot], axis=0).astype(jnp.bfloat16)
    count = jnp.sum(onehot(owners == cube, jnp.float32), axis=1, keepdims=True)
    live = onehot(count > (iota((8, 128), 1) // BLOCK).astype(jnp.float32), jnp.float32)
    source = (owners_f * 8.0 + rank).astype(jnp.int32)
    dest = dest_ref[...]
    child_owner, child_slot = [], []
    for q in range(4):
        row = dest[q : q + 1, :]
        at = onehot(iota((128, 128), 0) == row % 128)
        found = dot(table, at)
        mask = onehot(iota((8, 128), 0) == row // 128, jnp.float32)
        child_owner.append(jnp.sum(found[0:8] * mask, axis=0, keepdims=True))
        child_slot.append(jnp.sum(found[8:16] * mask, axis=0, keepdims=True))
    child_owner = jnp.concatenate(child_owner + child_owner, axis=0)
    child_slot = jnp.concatenate(child_slot + child_slot, axis=0)
    mine = jnp.where(child_owner == cube.astype(jnp.float32), child_slot + 1.0, 0.0)
    group = onehot(iota((128, 128), 0) // BLOCK == iota((128, 128), 1) // BLOCK)
    joined = dot(mine.astype(jnp.bfloat16), group)
    within = (iota((8, 128), 1) % BLOCK).astype(jnp.float32)
    place = jnp.where(joined > 0.5, (joined - 1.0) * BLOCK + within, -1.0).astype(jnp.int32)
    expand = onehot(iota((128, 256), 0) == (cube % 8) * BLOCK + iota((128, 256), 1) // BLOCK)
    own = dot(child_owner.astype(jnp.bfloat16), expand)
    own = jnp.sum(jnp.where(iota((8, 256), 0) == cube // 8, own, 0.0), axis=0, keepdims=True)
    spread = onehot(iota((16, 256), 1) % BLOCK == iota((16, 256), 0))
    rows = dot(rows_ref[...].astype(jnp.float32).astype(jnp.bfloat16), spread)
    rows = jnp.sum(jnp.where(iota((16, 256), 1) // BLOCK == iota((16, 256), 0), rows, 0.0), axis=0, keepdims=True)
    send = (own * BLOCK + rows).astype(jnp.int32)
    return send, place, live, source


def exchange(
    owner_ref,
    dest_ref,
    rows_ref,
    update_ref,
    panel_ref,
    entries_ref,
    inverse_ref,
    recv_update,
    col_factor,
    row_factor,
    place_ref,
    source_ref,
    send_update,
    send_panel,
    recv_panel,
    z_send,
    z_recv,
    piece,
    up_send,
    up_recv,
    pan_send,
    pan_recv,
    za_send,
    za_recv,
    zg_send,
    zg_recv,
    ag_send,
    ag_recv,
    local_sem,
):
    cube = lax.axis_index("cube")
    grid = lax.axis_index("grid")
    core, x, y = cube % 2, (cube // 2) % 4, cube // 8

    def peer(d):
        return ((y + d // 8) % 4 * 4 + (x + d // 2 % 4) % 4) * 2 + (core + d) % 2

    def origin(d):
        return ((y + 4 - d // 8) % 4 * 4 + (x + 4 - d // 2 % 4) % 4) * 2 + (core + d) % 2

    barrier = pltpu.get_barrier_semaphore()

    def greet(d, carry):
        pl.semaphore_signal(barrier, inc=1, device_id={"cube": peer(d)}, device_id_type=MESH)
        return carry

    lax.fori_loop(1, 32, greet, 0)

    def greet_z(d, carry):
        pl.semaphore_signal(barrier, inc=1, device_id={"grid": (grid + d) % 8}, device_id_type=MESH)
        return carry

    lax.fori_loop(1, 8, greet_z, 0)

    send, place, live, source = index_tables(cube, owner_ref, dest_ref, rows_ref)
    place_ref[...] = place
    source_ref[...] = source
    route = onehot(iota((512, 256), 0) == send)
    panel_in = jnp.concatenate([panel_ref[...], jnp.zeros((64, 256), jnp.bfloat16)], axis=0)
    send_panel[...] = dot_nt(route, panel_in).astype(jnp.bfloat16)
    for n in range(4):
        cols = slice(512 * n, 512 * n + 512)
        send_update[:, cols] = dot(route, update_ref[:, cols]).astype(jnp.bfloat16)

    def rows16(owner):
        return pl.ds(pl.multiple_of(owner * BLOCK, BLOCK), BLOCK)

    pl.semaphore_wait(barrier, 38)

    def panel_copy(d):
        to = peer(d)
        return pltpu.make_async_remote_copy(
            send_panel.at[rows16(to), :], recv_panel.at[rows16(cube), :],
            pan_send.at[d], pan_recv.at[d], device_id={"cube": to}, device_id_type=MESH,
        )

    def panel_wait(d):
        return pltpu.make_async_remote_copy(
            send_panel.at[rows16(peer(d)), :], recv_panel.at[rows16(origin(d)), :],
            pan_send.at[d], pan_recv.at[d], device_id={"cube": peer(d)}, device_id_type=MESH,
        )

    def update_copy(d):
        to = peer(d)
        return pltpu.make_async_remote_copy(
            send_update.at[rows16(to), :], recv_update.at[rows16(cube), :],
            up_send.at[d], up_recv.at[d], device_id={"cube": to}, device_id_type=MESH,
        )

    def update_wait(d):
        return pltpu.make_async_remote_copy(
            send_update.at[rows16(peer(d)), :], recv_update.at[rows16(origin(d)), :],
            up_send.at[d], up_recv.at[d], device_id={"cube": peer(d)}, device_id_type=MESH,
        )

    def run(low, high, step):
        def body(d, carry):
            step(d)
            return carry

        lax.fori_loop(low, high, body, 0)

    run(1, 32, lambda d: panel_copy(d).start())
    run(1, EARLY, lambda d: update_copy(d).start())
    own_update = pltpu.make_async_copy(
        send_update.at[rows16(cube), :], recv_update.at[rows16(cube), :], local_sem.at[0]
    )
    own_update.start()
    recv_panel[rows16(cube), :] = send_panel[rows16(cube), :]
    run(1, 32, lambda d: panel_wait(d).wait())

    panel_t = recv_panel[...].astype(jnp.float32).T.astype(jnp.bfloat16)
    for r in range(8):
        gather = jnp.concatenate(
            [onehot(iota((128, 128), 0) + r * 128 == place[q : q + 1, :]) for q in range(4)], axis=1
        )
        total = dot_nt(panel_t, gather)[0:64]
        entries = entries_ref[:, 128 * r : 128 * r + 128].astype(jnp.float32)
        total = total + jnp.where(live[r : r + 1, :] > 0.5, entries, 0.0)
        z_send[r] = total.astype(jnp.bfloat16)

    def zrows(g):
        return pl.ds(pl.multiple_of(g * 64, 64), 64)

    def z_copy(d, into):
        to = (grid + d) % 8
        return pltpu.make_async_remote_copy(
            z_send.at[to], z_recv.at[zrows(into), :],
            za_send.at[d], za_recv.at[d], device_id={"grid": to}, device_id_type=MESH,
        )

    run(1, 8, lambda d: z_copy(d, grid).start())
    z_recv[zrows(grid), :] = z_send[grid]
    run(1, 8, lambda d: z_copy(d, (grid + 8 - d) % 8).wait())
    front = z_recv[...].astype(jnp.float32).T.astype(jnp.bfloat16)
    piece[...] = dot(front, inverse_ref[...]).astype(jnp.bfloat16)

    a = x + core * (y - x)
    b = y + core * (x - y)

    def device(k, p, q):
        return ((q + k * (p - q)) * 4 + p + k * (q - p)) * 2 + k

    def stretch(owner, low, size):
        return pl.ds(pl.multiple_of(owner * PIECE + low, 64), size)

    parts = {"full": (0, 128), "top": (0, 64), "bottom": (64, 64)}

    def ag_copy(m, owner, part, to):
        low, size = parts[part]
        there = col_factor.at[stretch(owner, low, size), :]
        return pltpu.make_async_remote_copy(
            there, there, ag_send.at[m], ag_recv.at[m], device_id={"cube": to}, device_id_type=MESH
        )

    def ag_own(m, to):
        return pltpu.make_async_remote_copy(
            piece, col_factor.at[stretch(cube, 0, 128), :],
            ag_send.at[m], ag_recv.at[m], device_id={"cube": to}, device_id_type=MESH,
        )

    off = (0, 3, 1, 2)
    pa = [(a + o) % 4 for o in off]
    pb = [(b + o) % 4 for o in off]
    a_next, a_prev = device(core, pa[2], b), device(core, pa[1], b)
    b_next, b_prev = device(core, a, pb[2]), device(core, a, pb[1])
    sibling = cube + 1 - 2 * core
    sent = []

    def go(copy):
        copy.start()
        sent.append(copy)

    def got(m, owner, part):
        ag_copy(m, owner, part, a_next).wait_recv()

    def to_sibling(p, q):
        go(ag_copy(20 + 4 * p + q, device(core, pa[p], pb[q]), "full", sibling))

    def phase2(p):
        go(ag_copy(4 + 4 * p, device(core, pa[p], b), "full", b_next))
        go(ag_copy(5 + 4 * p, device(core, pa[p], b), "full", b_prev))
        to_sibling(p, 0)

    def near(p):
        below, above = device(core, pa[p], pb[1]), device(core, pa[p], pb[2])
        got(4 + 4 * p, below, "full")
        go(ag_copy(6 + 4 * p, below, "top", b_next))
        to_sibling(p, 1)
        got(5 + 4 * p, above, "full")
        go(ag_copy(7 + 4 * p, above, "bottom", b_prev))
        to_sibling(p, 2)

    def far(p):
        owner = device(core, pa[p], pb[3])
        got(6 + 4 * p, owner, "top")
        got(7 + 4 * p, owner, "bottom")
        to_sibling(p, 3)

    def z_part(m, owner, part, to):
        low, size = parts[part]
        there = row_factor.at[stretch(owner, low, size), :]
        return pltpu.make_async_remote_copy(
            there, there, zg_send.at[m], zg_recv.at[m], device_id={"grid": to}, device_id_type=MESH
        )

    def z_own(m, to):
        return pltpu.make_async_remote_copy(
            piece, row_factor.at[stretch(grid, 0, 128), :],
            zg_send.at[m], zg_recv.at[m], device_id={"grid": to}, device_id_type=MESH,
        )

    def gz(o):
        return (grid + 8 + o) % 8

    up, down = gz(1), gz(-1)

    def z_hop(k, part_up, part_down):
        z_part(2 * k - 2, gz(-k), "full", up).wait_recv()
        go(z_part(2 * k, gz(-k), part_up, up))
        z_part(2 * k - 1, gz(k), "full", up).wait_recv()
        go(z_part(2 * k + 1, gz(k), part_down, down))

    go(ag_own(0, a_next))
    go(ag_own(1, a_prev))
    go(z_own(0, up))
    go(z_own(1, down))
    go(ag_own(4, b_next))
    go(ag_own(5, b_prev))
    go(ag_own(20, sibling))
    own_col = pltpu.make_async_copy(piece, col_factor.at[stretch(cube, 0, 128), :], local_sem.at[1])
    own_row = pltpu.make_async_copy(piece, row_factor.at[stretch(grid, 0, 128), :], local_sem.at[2])
    own_col.start()
    own_row.start()
    run(EARLY, 32, lambda d: update_copy(d).start())

    left, right, across = device(core, pa[1], b), device(core, pa[2], b), device(core, pa[3], b)
    got(0, left, "full")
    go(ag_copy(2, left, "top", a_next))
    phase2(1)
    got(1, right, "full")
    go(ag_copy(3, right, "bottom", a_prev))
    phase2(2)
    z_hop(1, "full", "full")
    near(0)
    got(2, across, "top")
    got(3, across, "bottom")
    phase2(3)
    z_hop(2, "full", "full")
    near(1)
    far(0)
    near(2)
    z_hop(3, "top", "bottom")
    far(1)
    near(3)
    far(2)
    far(3)
    z_part(6, gz(4), "top", up).wait_recv()
    z_part(7, gz(4), "bottom", up).wait_recv()
    other = 1 - core
    oa = [(b + o) % 4 for o in off]
    ob = [(a + o) % 4 for o in off]
    for p in range(4):
        for q in range(4):
            got(20 + 4 * p + q, device(other, oa[p], ob[q]), "full")
    run(1, 32, lambda d: update_wait(d).wait())
    own_update.wait()
    own_col.wait()
    own_row.wait()
    for copy in sent:
        copy.wait_send()


def combine(source_ref, place_ref, recv_ref, row_ref, col_ref, out_ref, panel_ref, gather, columns):
    step = pl.program_id(0)
    grid = lax.axis_index("grid")
    width = out_ref.shape[1]

    @pl.when(step == 0)
    def _():
        for q in range(4):
            gather[:, 128 * q : 128 * q + 128] = onehot(iota((1024, 128), 0) == place_ref[q : q + 1, :])
        pick = onehot(iota((64, 512), 1) == grid * 64 + iota((64, 512), 0))
        panel_ref[...] = dot_nt(pick, row_ref[...]).astype(jnp.bfloat16)

    for n in range(width // BLOCK):
        source = source_ref[grid, step * (width // BLOCK) + n]
        columns[BLOCK * n : BLOCK * n + BLOCK, :] = col_ref[pl.ds(pl.multiple_of(source * BLOCK, BLOCK), BLOCK), :]
    total = dot(gather[...], recv_ref[...]) - dot_nt(row_ref[...], columns[...])
    out_ref[...] = total.astype(jnp.bfloat16)


def local(child_update, child_panel, panel_entries, panel_inverse, block_owner, child_dest, child_rows):
    vmem = pl.BlockSpec(memory_space=pltpu.VMEM)
    anywhere = pl.BlockSpec(memory_space=pl.ANY)
    bf16 = jnp.bfloat16
    dma = pltpu.SemaphoreType.DMA
    recv_update, col_factor, row_factor, place, source = pl.pallas_call(
        exchange,
        out_shape=(
            jax.ShapeDtypeStruct((512, 2048), bf16),
            jax.ShapeDtypeStruct((4096, 512), bf16),
            jax.ShapeDtypeStruct((1024, 512), bf16),
            jax.ShapeDtypeStruct((8, 128), jnp.int32),
            jax.ShapeDtypeStruct((8, 128), jnp.int32),
        ),
        in_specs=[vmem] * 7,
        out_specs=(anywhere, anywhere, anywhere, vmem, vmem),
        scratch_shapes=[
            pltpu.VMEM((512, 2048), bf16),
            pltpu.VMEM((512, 128), bf16),
            pltpu.VMEM((512, 128), bf16),
            pltpu.VMEM((8, 64, 128), bf16),
            pltpu.VMEM((512, 128), bf16),
            pltpu.VMEM((128, 512), bf16),
            dma((32,)), dma((32,)), dma((32,)), dma((32,)),
            dma((8,)), dma((8,)), dma((8,)), dma((8,)),
            dma((36,)), dma((36,)), dma((3,)),
        ],
        compiler_params=pltpu.CompilerParams(
            collective_id=0, has_side_effects=True, vmem_limit_bytes=24 * 1024 * 1024
        ),
        name="exchange",
    )(
        block_owner.reshape(8, 128), child_dest.reshape(4, 128), child_rows,
        child_update, child_panel, panel_entries, panel_inverse,
    )
    width = 256
    steps = 2048 // width
    out, panel = pl.pallas_call(
        combine,
        out_shape=(jax.ShapeDtypeStruct((1024, 2048), bf16), jax.ShapeDtypeStruct((64, 1024), bf16)),
        grid_spec=pltpu.PrefetchScalarGridSpec(
            num_scalar_prefetch=1,
            grid=(steps,),
            in_specs=[
                pl.BlockSpec((8, 128), lambda i, s: (0, 0)),
                pl.BlockSpec((512, width), lambda i, s: (0, i)),
                pl.BlockSpec((1024, 512), lambda i, s: (0, 0)),
                pl.BlockSpec((4096, 512), lambda i, s: (0, 0)),
            ],
            out_specs=[
                pl.BlockSpec((1024, width), lambda i, s: (0, i)),
                pl.BlockSpec((64, 1024), lambda i, s: (0, 0)),
            ],
            scratch_shapes=[pltpu.VMEM((1024, 512), bf16), pltpu.VMEM((width, 512), bf16)],
        ),
        compiler_params=pltpu.CompilerParams(
            dimension_semantics=("arbitrary",), vmem_limit_bytes=32 * 1024 * 1024
        ),
        name="combine",
    )(source, place, recv_update, row_factor, col_factor)
    return out, panel


def solution(mesh):
    placed = (
        P("cube", "grid"),
        P("grid", "cube"),
        P("grid", "cube"),
        P(),
        P(),
        P(),
        P("cube", None),
    )
    return jax.shard_map(
        local,
        mesh=mesh,
        in_specs=placed,
        out_specs=(P("cube", "grid"), P("grid", "cube")),
        check_vma=False,
    )
```

```python
import functools

import jax
import jax.numpy as jnp
from jax import lax
from jax.experimental import pallas as pl
from jax.experimental.pallas import tpu as pltpu
from jax.sharding import PartitionSpec as P

MESH = pl.DeviceIdType.MESH
BLOCK = 16
PIECE = 128
INJECT = (0, 8, 4, 2, 2, 4, 4, 31)
NEAR_FIRST = False
DIRECT2 = False
WIDTH = 512


def iota(shape, dim):
    return lax.broadcasted_iota(jnp.int32, shape, dim)


def onehot(cond, dtype=jnp.bfloat16):
    return jnp.where(cond, 1.0, 0.0).astype(dtype)


def dot(lhs, rhs):
    return jnp.dot(lhs, rhs, preferred_element_type=jnp.float32)


def dot_nt(lhs, rhs):
    return lax.dot_general(lhs, rhs, (((1,), (1,)), ((), ())), preferred_element_type=jnp.float32)


def hops(d):
    return min(d // 8, 4 - d // 8) + min(d // 2 % 4, 4 - d // 2 % 4)


ORDER = sorted(range(1, 32), key=hops if NEAR_FIRST else lambda d: -hops(d))


def index_tables(cube, owner_ref, dest_ref, rows_ref):
    owners = owner_ref[...]
    hot = jnp.concatenate(
        [onehot(iota((32, 128), 0) == owners[r : r + 1, :], jnp.float32) for r in range(8)], axis=0
    )
    before = onehot(iota((128, 128), 0) < iota((128, 128), 1))
    running = dot(hot.astype(jnp.bfloat16), before)
    picked = hot * running
    rank = jnp.concatenate(
        [jnp.sum(picked[32 * r : 32 * r + 32], axis=0, keepdims=True) for r in range(8)], axis=0
    )
    owners_f = owners.astype(jnp.float32)
    slot = rank + 8.0 * iota((8, 128), 0).astype(jnp.float32)
    table = jnp.concatenate([owners_f, slot], axis=0).astype(jnp.bfloat16)
    count = jnp.sum(onehot(owners == cube, jnp.float32), axis=1, keepdims=True)
    live = onehot(count > (iota((8, 128), 1) // BLOCK).astype(jnp.float32), jnp.float32)
    source = (owners_f * 8.0 + rank).astype(jnp.int32)
    dest = dest_ref[...]
    child_owner, child_slot = [], []
    for q in range(4):
        row = dest[q : q + 1, :]
        at = onehot(iota((128, 128), 0) == row % 128)
        found = dot(table, at)
        mask = onehot(iota((8, 128), 0) == row // 128, jnp.float32)
        child_owner.append(jnp.sum(found[0:8] * mask, axis=0, keepdims=True))
        child_slot.append(jnp.sum(found[8:16] * mask, axis=0, keepdims=True))
    child_owner = jnp.concatenate(child_owner + child_owner, axis=0)
    child_slot = jnp.concatenate(child_slot + child_slot, axis=0)
    mine = jnp.where(child_owner == cube.astype(jnp.float32), child_slot + 1.0, 0.0)
    group = onehot(iota((128, 128), 0) // BLOCK == iota((128, 128), 1) // BLOCK)
    joined = dot(mine.astype(jnp.bfloat16), group)
    within = (iota((8, 128), 1) % BLOCK).astype(jnp.float32)
    place = jnp.where(joined > 0.5, (joined - 1.0) * BLOCK + within, -1.0).astype(jnp.int32)
    expand = onehot(iota((128, 256), 0) == (cube % 8) * BLOCK + iota((128, 256), 1) // BLOCK)
    own = dot(child_owner.astype(jnp.bfloat16), expand)
    own = jnp.sum(jnp.where(iota((8, 256), 0) == cube // 8, own, 0.0), axis=0, keepdims=True)
    spread = onehot(iota((16, 256), 1) % BLOCK == iota((16, 256), 0))
    rows = dot(rows_ref[...].astype(jnp.float32).astype(jnp.bfloat16), spread)
    rows = jnp.sum(jnp.where(iota((16, 256), 1) // BLOCK == iota((16, 256), 0), rows, 0.0), axis=0, keepdims=True)
    send = (own * BLOCK + rows).astype(jnp.int32)
    return send, place, live, source


def exchange(
    owner_hbm,
    dest_hbm,
    rows_hbm,
    panel_hbm,
    update_hbm,
    entries_hbm,
    inverse_hbm,
    recv_update,
    col_factor,
    row_factor,
    place_ref,
    source_ref,
    send_update,
    send_panel,
    recv_panel,
    z_send,
    z_recv,
    piece,
    up_send,
    up_recv,
    pan_send,
    pan_recv,
    za_send,
    za_recv,
    zg_send,
    zg_recv,
    ag_send,
    ag_recv,
    local_sem,
    load_sem,
    owner_ref,
    dest_ref,
    rows_ref,
    panel_ref,
    update_ref,
    entries_ref,
    inverse_ref,
):
    sources = (owner_hbm, dest_hbm, rows_hbm, panel_hbm, update_hbm, entries_hbm, inverse_hbm)
    targets = (owner_ref, dest_ref, rows_ref, panel_ref, update_ref, entries_ref, inverse_ref)
    loads = [
        pltpu.make_async_copy(source, target, load_sem.at[n])
        for n, (source, target) in enumerate(zip(sources, targets))
    ]
    for load in loads:
        load.start()
    cube = lax.axis_index("cube")
    grid = lax.axis_index("grid")
    core, x, y = cube % 2, (cube // 2) % 4, cube // 8

    def peer(d):
        return ((y + d // 8) % 4 * 4 + (x + d // 2 % 4) % 4) * 2 + (core + d) % 2

    def origin(d):
        return ((y + 4 - d // 8) % 4 * 4 + (x + 4 - d // 2 % 4) % 4) * 2 + (core + d) % 2

    barrier = pltpu.get_barrier_semaphore()

    def greet(d, carry):
        pl.semaphore_signal(barrier, inc=1, device_id={"cube": peer(d)}, device_id_type=MESH)
        return carry

    lax.fori_loop(1, 32, greet, 0)

    def greet_z(d, carry):
        pl.semaphore_signal(barrier, inc=1, device_id={"grid": (grid + d) % 8}, device_id_type=MESH)
        return carry

    lax.fori_loop(1, 8, greet_z, 0)

    for load in loads[:3]:
        load.wait()
    send, place, live, source = index_tables(cube, owner_ref, dest_ref, rows_ref)
    place_ref[...] = place
    source_ref[...] = source
    route = onehot(iota((512, 256), 0) == send)
    loads[3].wait()
    panel_in = jnp.concatenate([panel_ref[...], jnp.zeros((64, 256), jnp.bfloat16)], axis=0)
    send_panel[...] = dot_nt(route, panel_in).astype(jnp.bfloat16)
    loads[4].wait()
    for n in range(4):
        cols = slice(512 * n, 512 * n + 512)
        send_update[:, cols] = dot(route, update_ref[:, cols]).astype(jnp.bfloat16)

    def rows16(owner):
        return pl.ds(pl.multiple_of(owner * BLOCK, BLOCK), BLOCK)

    pl.semaphore_wait(barrier, 38)

    def panel_copy(d):
        to = peer(d)
        return pltpu.make_async_remote_copy(
            send_panel.at[rows16(to), :], recv_panel.at[rows16(cube), :],
            pan_send.at[d], pan_recv.at[d], device_id={"cube": to}, device_id_type=MESH,
        )

    def panel_wait(d):
        return pltpu.make_async_remote_copy(
            send_panel.at[rows16(peer(d)), :], recv_panel.at[rows16(origin(d)), :],
            pan_send.at[d], pan_recv.at[d], device_id={"cube": peer(d)}, device_id_type=MESH,
        )

    def update_copy(d):
        to = peer(d)
        return pltpu.make_async_remote_copy(
            send_update.at[rows16(to), :], recv_update.at[rows16(cube), :],
            up_send.at[d], up_recv.at[d], device_id={"cube": to}, device_id_type=MESH,
        )

    def update_wait(d):
        return pltpu.make_async_remote_copy(
            send_update.at[rows16(peer(d)), :], recv_update.at[rows16(origin(d)), :],
            up_send.at[d], up_recv.at[d], device_id={"cube": peer(d)}, device_id_type=MESH,
        )

    def run(low, high, step):
        def body(d, carry):
            step(d)
            return carry

        lax.fori_loop(low, high, body, 0)

    run(1, 32, lambda d: panel_copy(d).start())
    pending = list(ORDER)
    stage = iter(INJECT)

    def inject():
        count = next(stage)
        for d in pending[:count]:
            update_copy(d).start()
        del pending[:count]

    inject()
    own_update = pltpu.make_async_copy(
        send_update.at[rows16(cube), :], recv_update.at[rows16(cube), :], local_sem.at[0]
    )
    own_update.start()
    recv_panel[rows16(cube), :] = send_panel[rows16(cube), :]
    run(1, 32, lambda d: panel_wait(d).wait())
    inject()

    loads[5].wait()
    loads[6].wait()
    panel_t = recv_panel[...].astype(jnp.float32).T.astype(jnp.bfloat16)
    for r in range(8):
        gather = jnp.concatenate(
            [onehot(iota((128, 128), 0) + r * 128 == place[q : q + 1, :]) for q in range(4)], axis=1
        )
        total = dot_nt(panel_t, gather)[0:64]
        entries = entries_ref[:, 128 * r : 128 * r + 128].astype(jnp.float32)
        total = total + jnp.where(live[r : r + 1, :] > 0.5, entries, 0.0)
        z_send[r] = total.astype(jnp.bfloat16)

    def zrows(g):
        return pl.ds(pl.multiple_of(g * 64, 64), 64)

    def z_copy(d, into):
        to = (grid + d) % 8
        return pltpu.make_async_remote_copy(
            z_send.at[to], z_recv.at[zrows(into), :],
            za_send.at[d], za_recv.at[d], device_id={"grid": to}, device_id_type=MESH,
        )

    run(1, 8, lambda d: z_copy(d, grid).start())
    z_recv[zrows(grid), :] = z_send[grid]
    run(1, 8, lambda d: z_copy(d, (grid + 8 - d) % 8).wait())
    front = z_recv[...].astype(jnp.float32).T.astype(jnp.bfloat16)
    piece[...] = dot(front, inverse_ref[...]).astype(jnp.bfloat16)

    a = x + core * (y - x)
    b = y + core * (x - y)

    def device(k, p, q):
        return ((q + k * (p - q)) * 4 + p + k * (q - p)) * 2 + k

    def stretch(owner, low, size):
        return pl.ds(pl.multiple_of(owner * PIECE + low, 64), size)

    parts = {"full": (0, 128), "top": (0, 64), "bottom": (64, 64)}

    def ag_copy(m, owner, part, to):
        low, size = parts[part]
        there = col_factor.at[stretch(owner, low, size), :]
        return pltpu.make_async_remote_copy(
            there, there, ag_send.at[m], ag_recv.at[m], device_id={"cube": to}, device_id_type=MESH
        )

    def ag_own(m, to):
        return pltpu.make_async_remote_copy(
            piece, col_factor.at[stretch(cube, 0, 128), :],
            ag_send.at[m], ag_recv.at[m], device_id={"cube": to}, device_id_type=MESH,
        )

    off = (0, 3, 1, 2)
    pa = [(a + o) % 4 for o in off]
    pb = [(b + o) % 4 for o in off]
    a_next, a_prev = device(core, pa[2], b), device(core, pa[1], b)
    b_next, b_prev = device(core, a, pb[2]), device(core, a, pb[1])
    b_far = device(core, a, pb[3])
    sibling = cube + 1 - 2 * core
    sent = []

    def go(copy):
        copy.start()
        sent.append(copy)

    def got(m, owner, part):
        ag_copy(m, owner, part, a_next).wait_recv()

    def to_sibling(p, q):
        go(ag_copy(20 + 4 * p + q, device(core, pa[p], pb[q]), "full", sibling))

    def phase2(p):
        go(ag_copy(4 + 4 * p, device(core, pa[p], b), "full", b_next))
        go(ag_copy(5 + 4 * p, device(core, pa[p], b), "full", b_prev))
        if DIRECT2:
            go(ag_copy(6 + 4 * p, device(core, pa[p], b), "full", b_far))
        to_sibling(p, 0)

    def near(p):
        below, above = device(core, pa[p], pb[1]), device(core, pa[p], pb[2])
        got(4 + 4 * p, below, "full")
        if not DIRECT2:
            go(ag_copy(6 + 4 * p, below, "top", b_next))
        to_sibling(p, 1)
        got(5 + 4 * p, above, "full")
        if not DIRECT2:
            go(ag_copy(7 + 4 * p, above, "bottom", b_prev))
        to_sibling(p, 2)

    def far(p):
        owner = device(core, pa[p], pb[3])
        if DIRECT2:
            got(6 + 4 * p, owner, "full")
        else:
            got(6 + 4 * p, owner, "top")
            got(7 + 4 * p, owner, "bottom")
        to_sibling(p, 3)

    def z_part(m, owner, part, to):
        low, size = parts[part]
        there = row_factor.at[stretch(owner, low, size), :]
        return pltpu.make_async_remote_copy(
            there, there, zg_send.at[m], zg_recv.at[m], device_id={"grid": to}, device_id_type=MESH
        )

    def z_own(m, to):
        return pltpu.make_async_remote_copy(
            piece, row_factor.at[stretch(grid, 0, 128), :],
            zg_send.at[m], zg_recv.at[m], device_id={"grid": to}, device_id_type=MESH,
        )

    def gz(o):
        return (grid + 8 + o) % 8

    up, down = gz(1), gz(-1)

    def z_hop(k, part_up, part_down):
        z_part(2 * k - 2, gz(-k), "full", up).wait_recv()
        go(z_part(2 * k, gz(-k), part_up, up))
        z_part(2 * k - 1, gz(k), "full", up).wait_recv()
        go(z_part(2 * k + 1, gz(k), part_down, down))

    go(ag_own(0, a_next))
    go(ag_own(1, a_prev))
    go(ag_own(2, device(core, pa[3], b)))
    go(z_own(0, up))
    go(z_own(1, down))
    go(ag_own(4, b_next))
    go(ag_own(5, b_prev))
    if DIRECT2:
        go(ag_own(6, b_far))
    go(ag_own(20, sibling))
    own_col = pltpu.make_async_copy(piece, col_factor.at[stretch(cube, 0, 128), :], local_sem.at[1])
    own_row = pltpu.make_async_copy(piece, row_factor.at[stretch(grid, 0, 128), :], local_sem.at[2])
    own_col.start()
    own_row.start()
    inject()

    left, right, across = device(core, pa[1], b), device(core, pa[2], b), device(core, pa[3], b)
    got(0, left, "full")
    phase2(1)
    inject()
    got(1, right, "full")
    phase2(2)
    inject()
    got(2, across, "full")
    phase2(3)
    inject()
    z_hop(1, "full", "full")
    near(0)
    inject()
    near(1)
    z_hop(2, "full", "full")
    near(2)
    inject()
    assert not pending
    far(0)
    near(3)
    z_hop(3, "top", "bottom")
    far(1)
    far(2)
    far(3)
    z_part(6, gz(4), "top", up).wait_recv()
    z_part(7, gz(4), "bottom", up).wait_recv()
    other = 1 - core
    oa = [(b + o) % 4 for o in off]
    ob = [(a + o) % 4 for o in off]
    for p in range(4):
        for q in range(4):
            got(20 + 4 * p + q, device(other, oa[p], ob[q]), "full")
    run(1, 32, lambda d: update_wait(d).wait())
    own_update.wait()
    own_col.wait()
    own_row.wait()
    for copy in sent:
        copy.wait_send()


def combine(source_ref, place_ref, recv_ref, row_ref, col_ref, out_ref, panel_ref, gather, columns):
    step = pl.program_id(0)
    grid = lax.axis_index("grid")
    width = out_ref.shape[1]

    @pl.when(step == 0)
    def _():
        for q in range(4):
            gather[:, 128 * q : 128 * q + 128] = onehot(iota((1024, 128), 0) == place_ref[q : q + 1, :])
        pick = onehot(iota((64, 512), 1) == grid * 64 + iota((64, 512), 0))
        panel_ref[...] = dot_nt(pick, row_ref[...]).astype(jnp.bfloat16)

    for n in range(width // BLOCK):
        source = source_ref[grid, step * (width // BLOCK) + n]
        columns[BLOCK * n : BLOCK * n + BLOCK, :] = col_ref[pl.ds(pl.multiple_of(source * BLOCK, BLOCK), BLOCK), :]
    total = dot(gather[...], recv_ref[:, pl.ds(pl.multiple_of(step * width, 128), width)]) - dot_nt(row_ref[...], columns[...])
    out_ref[...] = total.astype(jnp.bfloat16)


def local(child_update, child_panel, panel_entries, panel_inverse, block_owner, child_dest, child_rows):
    vmem = pl.BlockSpec(memory_space=pltpu.VMEM)
    anywhere = pl.BlockSpec(memory_space=pl.ANY)
    bf16 = jnp.bfloat16
    dma = pltpu.SemaphoreType.DMA
    recv_update, col_factor, row_factor, place, source = pl.pallas_call(
        exchange,
        out_shape=(
            jax.ShapeDtypeStruct((512, 2048), bf16),
            jax.ShapeDtypeStruct((4096, 512), bf16),
            jax.ShapeDtypeStruct((1024, 512), bf16),
            jax.ShapeDtypeStruct((8, 128), jnp.int32),
            jax.ShapeDtypeStruct((8, 128), jnp.int32),
        ),
        in_specs=[pl.BlockSpec(memory_space=pltpu.HBM)] * 7,
        out_specs=(anywhere, anywhere, anywhere, vmem, vmem),
        scratch_shapes=[
            pltpu.VMEM((512, 2048), bf16),
            pltpu.VMEM((512, 128), bf16),
            pltpu.VMEM((512, 128), bf16),
            pltpu.VMEM((8, 64, 128), bf16),
            pltpu.VMEM((512, 128), bf16),
            pltpu.VMEM((128, 512), bf16),
            dma((32,)), dma((32,)), dma((32,)), dma((32,)),
            dma((8,)), dma((8,)), dma((8,)), dma((8,)),
            dma((36,)), dma((36,)), dma((3,)), dma((7,)),
            pltpu.VMEM((8, 128), jnp.int32),
            pltpu.VMEM((4, 128), jnp.int32),
            pltpu.VMEM((16, 16), jnp.int32),
            pltpu.VMEM((64, 256), bf16),
            pltpu.VMEM((256, 2048), bf16),
            pltpu.VMEM((64, 1024), bf16),
            pltpu.VMEM((512, 512), bf16),
        ],
        compiler_params=pltpu.CompilerParams(
            collective_id=0, has_side_effects=True, vmem_limit_bytes=26 * 1024 * 1024
        ),
        name="exchange",
    )(
        *(
            pltpu.with_memory_space_constraint(operand, pltpu.HBM)
            for operand in (
                block_owner.reshape(8, 128), child_dest.reshape(4, 128), child_rows,
                child_panel, child_update, panel_entries, panel_inverse,
            )
        )
    )
    width = WIDTH
    steps = 2048 // width
    out, panel = pl.pallas_call(
        combine,
        out_shape=(jax.ShapeDtypeStruct((1024, 2048), bf16), jax.ShapeDtypeStruct((64, 1024), bf16)),
        grid_spec=pltpu.PrefetchScalarGridSpec(
            num_scalar_prefetch=1,
            grid=(steps,),
            in_specs=[vmem] * 4,
            out_specs=[
                pl.BlockSpec((1024, width), lambda i, s: (0, i)),
                pl.BlockSpec((64, 1024), lambda i, s: (0, 0)),
            ],
            scratch_shapes=[pltpu.VMEM((1024, 512), bf16), pltpu.VMEM((width, 512), bf16)],
        ),
        compiler_params=pltpu.CompilerParams(
            dimension_semantics=("arbitrary",), vmem_limit_bytes=32 * 1024 * 1024
        ),
        name="combine",
    )(source, place, recv_update, row_factor, col_factor)
    return out, panel


def solution(mesh):
    placed = (
        P("cube", "grid"),
        P("grid", "cube"),
        P("grid", "cube"),
        P(),
        P(),
        P(),
        P("cube", None),
    )
    return jax.shard_map(
        local,
        mesh=mesh,
        in_specs=placed,
        out_specs=(P("cube", "grid"), P("grid", "cube")),
        check_vma=False,
    )
```

```python
import functools

import jax
import jax.numpy as jnp
from jax import lax
from jax.experimental import pallas as pl
from jax.experimental.pallas import tpu as pltpu
from jax.sharding import PartitionSpec as P

MESH = pl.DeviceIdType.MESH
BLOCK = 16
PIECE = 128
INJECT = (0, 8, 1, 1, 1, 2, 2, 31)
NEAR_FIRST = False
DIRECT2 = (False, False, False, True)
WIDTH = 512
START = 16


def iota(shape, dim):
    return lax.broadcasted_iota(jnp.int32, shape, dim)


def onehot(cond, dtype=jnp.bfloat16):
    return jnp.where(cond, 1.0, 0.0).astype(dtype)


def dot(lhs, rhs):
    return jnp.dot(lhs, rhs, preferred_element_type=jnp.float32)


def dot_nt(lhs, rhs):
    return lax.dot_general(lhs, rhs, (((1,), (1,)), ((), ())), preferred_element_type=jnp.float32)


def hops(d):
    return min(d // 8, 4 - d // 8) + min(d // 2 % 4, 4 - d // 2 % 4)


ORDER = sorted(range(1, 32), key=hops if NEAR_FIRST else lambda d: -hops(d))
SLOT = {d: n + 1 for n, d in enumerate(ORDER)}
SLOT[0] = 0


def send_tables(cube, owner_ref, dest_ref, rows_ref):
    owners = owner_ref[...]
    hot = jnp.concatenate(
        [onehot(iota((32, 128), 0) == owners[r : r + 1, :], jnp.float32) for r in range(8)], axis=0
    )
    before = onehot(iota((128, 128), 0) < iota((128, 128), 1))
    running = dot(hot.astype(jnp.bfloat16), before)
    picked = hot * running
    rank = jnp.concatenate(
        [jnp.sum(picked[32 * r : 32 * r + 32], axis=0, keepdims=True) for r in range(8)], axis=0
    )
    owners_f = owners.astype(jnp.float32)
    slot = rank + 8.0 * iota((8, 128), 0).astype(jnp.float32)
    table = jnp.concatenate([owners_f, slot], axis=0).astype(jnp.bfloat16)
    count = jnp.sum(onehot(owners == cube, jnp.float32), axis=1, keepdims=True)
    live = onehot(count > (iota((8, 128), 1) // BLOCK).astype(jnp.float32), jnp.float32)
    dest = dest_ref[...]
    child_owner, child_slot = [], []
    for q in range(4):
        row = dest[q : q + 1, :]
        at = onehot(iota((128, 128), 0) == row % 128)
        found = dot(table, at)
        mask = onehot(iota((8, 128), 0) == row // 128, jnp.float32)
        child_owner.append(jnp.sum(found[0:8] * mask, axis=0, keepdims=True))
        child_slot.append(jnp.sum(found[8:16] * mask, axis=0, keepdims=True))
    child_owner = jnp.concatenate(child_owner + child_owner, axis=0)
    child_slot = jnp.concatenate(child_slot + child_slot, axis=0)
    expand = onehot(iota((128, 256), 0) == (cube % 8) * BLOCK + iota((128, 256), 1) // BLOCK)
    own = dot(child_owner.astype(jnp.bfloat16), expand)
    own = jnp.sum(jnp.where(iota((8, 256), 0) == cube // 8, own, 0.0), axis=0, keepdims=True)
    spread = onehot(iota((16, 256), 1) % BLOCK == iota((16, 256), 0))
    rows = dot(rows_ref[...].astype(jnp.float32).astype(jnp.bfloat16), spread)
    rows = jnp.sum(jnp.where(iota((16, 256), 1) // BLOCK == iota((16, 256), 0), rows, 0.0), axis=0, keepdims=True)
    send = (own * BLOCK + rows).astype(jnp.int32)
    return send, live, child_owner, child_slot


def receive_table(cube, origins, child_owner, child_slot):
    mine = jnp.where(child_owner == cube.astype(jnp.float32), child_slot + 1.0, 0.0).astype(jnp.bfloat16)
    places = []
    for q in range(4):
        lane = iota((1, 128), 1) // BLOCK
        wanted = jnp.zeros((1, 128), jnp.int32)
        for n in range(8):
            wanted = jnp.where(lane == n, origins[8 * q + n], wanted)
        joined = jnp.zeros((8, 128), jnp.float32)
        for p in range(4):
            pick = onehot(iota((128, 128), 0) // BLOCK + 8 * p == wanted)
            part = dot(mine, pick)
            joined = joined + jnp.where(iota((8, 128), 0) == p, part, 0.0)
        joined = jnp.sum(joined, axis=0, keepdims=True)
        within = (iota((1, 128), 1) % BLOCK).astype(jnp.float32)
        places.append(jnp.where(joined > 0.5, (joined - 1.0) * BLOCK + within, -1.0).astype(jnp.int32))
    return places


def exchange(
    owner_hbm,
    dest_hbm,
    rows_hbm,
    panel_hbm,
    update_hbm,
    entries_hbm,
    inverse_hbm,
    recv_update,
    row_factor,
    gather_ref,
    partial,
    col_factor,
    source_ref,
    source_smem,
    owner_smem,
    columns,
    send_update,
    send_panel,
    recv_panel,
    z_send,
    z_recv,
    piece,
    blocks,
    up_send,
    up_recv,
    pan_send,
    pan_recv,
    za_send,
    za_recv,
    zg_send,
    zg_recv,
    ag_send,
    ag_recv,
    local_sem,
    load_sem,
    owner_ref,
    dest_ref,
    rows_ref,
    panel_ref,
    update_ref,
    entries_ref,
    inverse_ref,
):
    sources = (owner_hbm, dest_hbm, rows_hbm, panel_hbm, update_hbm, entries_hbm, inverse_hbm)
    targets = (owner_ref, dest_ref, rows_ref, panel_ref, update_ref, entries_ref, inverse_ref)
    loads = [
        pltpu.make_async_copy(source, target, load_sem.at[n])
        for n, (source, target) in enumerate(zip(sources, targets))
    ]
    for load in loads:
        load.start()
    to_owners = pltpu.make_async_copy(owner_hbm, owner_smem, local_sem.at[4])
    to_owners.start()
    cube = lax.axis_index("cube")
    grid = lax.axis_index("grid")
    core, x, y = cube % 2, (cube // 2) % 4, cube // 8

    ys = [8 * ((y + k) % 4) for k in range(4)]
    xs = [2 * ((x + k) % 4) for k in range(4)]
    cores = [core, 1 - core]

    def peer(d):
        return ys[d // 8] + xs[d // 2 % 4] + cores[d % 2]

    def origin(d):
        return ys[-(d // 8) % 4] + xs[-(d // 2 % 4) % 4] + cores[d % 2]

    barrier = pltpu.get_barrier_semaphore()

    for d in sorted(range(1, 32), key=hops, reverse=True):
        pl.semaphore_signal(barrier, inc=1, device_id={"cube": peer(d)}, device_id_type=MESH)
    for d in (4, 3, 5, 2, 6, 1, 7):
        pl.semaphore_signal(barrier, inc=1, device_id={"grid": (grid + d) % 8}, device_id_type=MESH)

    for load in loads[:3]:
        load.wait()
    send, live, child_owner, child_slot = send_tables(cube, owner_ref, dest_ref, rows_ref)
    route = onehot(iota((512, 256), 0) == send)
    loads[3].wait()
    panel_in = jnp.concatenate([panel_ref[...], jnp.zeros((64, 256), jnp.bfloat16)], axis=0)
    send_panel[...] = dot_nt(route, panel_in).astype(jnp.bfloat16)

    def rows16(owner):
        return pl.ds(pl.multiple_of(owner * BLOCK, BLOCK), BLOCK)

    def slot16(d):
        return pl.ds(BLOCK * SLOT[d], BLOCK)

    pl.semaphore_wait(barrier, 38)

    def panel_copy(d):
        to = peer(d)
        return pltpu.make_async_remote_copy(
            send_panel.at[rows16(to), :], recv_panel.at[slot16(d), :],
            pan_send.at[d], pan_recv.at[d], device_id={"cube": to}, device_id_type=MESH,
        )

    def panel_wait(d):
        return pltpu.make_async_remote_copy(
            send_panel.at[rows16(peer(d)), :], recv_panel.at[slot16(d), :],
            pan_send.at[d], pan_recv.at[d], device_id={"cube": peer(d)}, device_id_type=MESH,
        )

    def update_copy(d):
        to = peer(d)
        return pltpu.make_async_remote_copy(
            send_update.at[rows16(to), :], recv_update.at[slot16(d), :],
            up_send.at[d], up_recv.at[d], device_id={"cube": to}, device_id_type=MESH,
        )

    def update_wait(d):
        return pltpu.make_async_remote_copy(
            send_update.at[rows16(peer(d)), :], recv_update.at[slot16(d), :],
            up_send.at[d], up_recv.at[d], device_id={"cube": peer(d)}, device_id_type=MESH,
        )

    far_first = sorted(range(1, 32), key=hops, reverse=True)
    for d in far_first:
        panel_copy(d).start()
    loads[4].wait()
    for n in range(4):
        cols = slice(512 * n, 512 * n + 512)
        send_update[:, cols] = dot(route, update_ref[:, cols]).astype(jnp.bfloat16)
    by_slot = {n: d for d, n in SLOT.items()}
    to_owners.wait()
    range_owner = owner_ref[pl.ds(grid, 1), :]
    range_rank = jnp.zeros((1, 128), jnp.int32)
    for n in range(127):
        earlier = (range_owner == owner_smem[grid, n]) & (iota((1, 128), 1) > n)
        range_rank = range_rank + jnp.where(earlier, 1, 0)
    source_ref[...] = range_owner * 8 + range_rank
    places = receive_table(cube, [origin(by_slot[n]) for n in range(32)], child_owner, child_slot)
    pending = list(ORDER)
    stage = iter(INJECT)

    def inject():
        count = next(stage)
        for d in pending[:count]:
            update_copy(d).start()
        del pending[:count]

    inject()
    own_update = pltpu.make_async_copy(
        send_update.at[rows16(cube), :], recv_update.at[slot16(0), :], local_sem.at[0]
    )
    own_update.start()
    recv_panel[slot16(0), :] = send_panel[rows16(cube), :]
    for d in far_first:
        panel_wait(d).wait()
    inject()

    loads[5].wait()
    loads[6].wait()
    panel_t = recv_panel[...].astype(jnp.float32).T.astype(jnp.bfloat16)
    for r in range(8):
        gather = jnp.concatenate(
            [onehot(iota((128, 128), 0) + r * 128 == places[q]) for q in range(4)], axis=1
        )
        gather_ref[128 * r : 128 * r + 128, :] = gather
        total = dot_nt(panel_t, gather)[0:64]
        entries = entries_ref[:, 128 * r : 128 * r + 128].astype(jnp.float32)
        total = total + jnp.where(live[r : r + 1, :] > 0.5, entries, 0.0)
        z_send[r] = total.astype(jnp.bfloat16)

    def zrows(g):
        return pl.ds(pl.multiple_of(g * 64, 64), 64)

    def z_copy(d, into):
        to = (grid + d) % 8
        return pltpu.make_async_remote_copy(
            z_send.at[to], z_recv.at[zrows(into), :],
            za_send.at[d], za_recv.at[d], device_id={"grid": to}, device_id_type=MESH,
        )

    for d in (4, 3, 5, 2, 6, 1, 7):
        z_copy(d, grid).start()
    z_recv[zrows(grid), :] = z_send[grid]
    for d in (4, 3, 5, 2, 6, 1, 7):
        z_copy(d, (grid + 8 - d) % 8).wait()
    front = z_recv[...].astype(jnp.float32).T.astype(jnp.bfloat16)
    own_factor = dot(front, inverse_ref[...]).astype(jnp.bfloat16)
    piece[...] = own_factor
    blocks[...] = own_factor.reshape(8, BLOCK, 512)

    a = x + core * (y - x)
    b = y + core * (x - y)

    def device(k, p, q):
        return ((q + k * (p - q)) * 4 + p + k * (q - p)) * 2 + k

    def stretch(owner, low, size):
        return pl.ds(pl.multiple_of(owner * PIECE + low, 64), size)

    parts = {"full": (0, 128), "top": (0, 64), "bottom": (64, 64)}

    def ag_copy(m, owner, part, to):
        low, size = parts[part]
        there = col_factor.at[pl.ds(owner * 8 + low // BLOCK, size // BLOCK)]
        return pltpu.make_async_remote_copy(
            there, there, ag_send.at[m], ag_recv.at[m], device_id={"cube": to}, device_id_type=MESH
        )

    def ag_own(m, to):
        return pltpu.make_async_remote_copy(
            blocks, col_factor.at[pl.ds(cube * 8, 8)],
            ag_send.at[m], ag_recv.at[m], device_id={"cube": to}, device_id_type=MESH,
        )

    off = (0, 3, 1, 2)
    pa = [(a + o) % 4 for o in off]
    pb = [(b + o) % 4 for o in off]
    a_next, a_prev = device(core, pa[2], b), device(core, pa[1], b)
    b_next, b_prev = device(core, a, pb[2]), device(core, a, pb[1])
    b_far = device(core, a, pb[3])
    sibling = cube + 1 - 2 * core
    sent = []

    def go(copy):
        copy.start()
        sent.append(copy)

    def got(m, owner, part):
        ag_copy(m, owner, part, a_next).wait_recv()

    def to_sibling(p, q):
        go(ag_copy(20 + 4 * p + q, device(core, pa[p], pb[q]), "full", sibling))

    def phase2(p):
        go(ag_copy(4 + 4 * p, device(core, pa[p], b), "full", b_next))
        go(ag_copy(5 + 4 * p, device(core, pa[p], b), "full", b_prev))
        if DIRECT2[p]:
            go(ag_copy(6 + 4 * p, device(core, pa[p], b), "full", b_far))
        to_sibling(p, 0)

    def near(p):
        below, above = device(core, pa[p], pb[1]), device(core, pa[p], pb[2])
        got(4 + 4 * p, below, "full")
        if not DIRECT2[p]:
            go(ag_copy(6 + 4 * p, below, "top", b_next))
        to_sibling(p, 1)
        got(5 + 4 * p, above, "full")
        if not DIRECT2[p]:
            go(ag_copy(7 + 4 * p, above, "bottom", b_prev))
        to_sibling(p, 2)

    def far(p):
        owner = device(core, pa[p], pb[3])
        if DIRECT2[p]:
            got(6 + 4 * p, owner, "full")
        else:
            got(6 + 4 * p, owner, "top")
            got(7 + 4 * p, owner, "bottom")
        to_sibling(p, 3)

    def z_part(m, owner, part, to):
        low, size = parts[part]
        there = row_factor.at[stretch(owner, low, size), :]
        return pltpu.make_async_remote_copy(
            there, there, zg_send.at[m], zg_recv.at[m], device_id={"grid": to}, device_id_type=MESH
        )

    def z_own(m, to):
        return pltpu.make_async_remote_copy(
            piece, row_factor.at[stretch(grid, 0, 128), :],
            zg_send.at[m], zg_recv.at[m], device_id={"grid": to}, device_id_type=MESH,
        )

    def gz(o):
        return (grid + 8 + o) % 8

    def z_got(m, owner, part):
        z_part(m, owner, part, gz(1)).wait_recv()

    def z_relay():
        z_got(2, gz(-2), "full")
        go(z_part(4, gz(-2), "full", gz(1)))
        go(z_part(6, gz(-2), "top", gz(2)))
        z_got(3, gz(2), "full")
        go(z_part(5, gz(2), "full", gz(-1)))
        go(z_part(7, gz(2), "bottom", gz(-2)))

    go(ag_own(0, a_next))
    go(ag_own(1, a_prev))
    go(ag_own(2, device(core, pa[3], b)))
    go(z_own(2, gz(2)))
    go(z_own(3, gz(-2)))
    go(z_own(0, gz(1)))
    go(z_own(1, gz(-1)))
    go(ag_own(4, b_next))
    go(ag_own(5, b_prev))
    if DIRECT2[0]:
        go(ag_own(6, b_far))
    go(ag_own(20, sibling))
    own_col = pltpu.make_async_copy(blocks, col_factor.at[pl.ds(cube * 8, 8)], local_sem.at[1])
    own_row = pltpu.make_async_copy(piece, row_factor.at[stretch(grid, 0, 128), :], local_sem.at[2])
    own_col.start()
    to_smem = pltpu.make_async_copy(source_ref, source_smem, local_sem.at[3])
    to_smem.start()
    own_row.start()
    inject()

    left, right, across = device(core, pa[1], b), device(core, pa[2], b), device(core, pa[3], b)
    got(0, left, "full")
    phase2(1)
    inject()
    got(1, right, "full")
    phase2(2)
    inject()
    near(0)
    got(2, across, "full")
    phase2(3)
    inject()
    z_relay()
    near(1)
    inject()
    near(2)
    far(0)
    near(3)
    inject()
    assert not pending
    far(1)
    far(2)
    far(3)
    for d in ORDER[: START - 1]:
        update_wait(d).wait()
    own_update.wait()
    head = BLOCK * START
    for n in range(8):
        cols = slice(256 * n, 256 * n + 256)
        partial[:, cols] = dot(gather_ref[:, 0:head], recv_update[0:head, cols])
    z_got(0, gz(-1), "full")
    z_got(1, gz(1), "full")
    z_got(4, gz(-3), "full")
    z_got(5, gz(3), "full")
    z_got(6, gz(4), "top")
    z_got(7, gz(4), "bottom")
    other = 1 - core
    oa = [(b + o) % 4 for o in off]
    ob = [(a + o) % 4 for o in off]
    for p in range(4):
        for q in range(4):
            got(20 + 4 * p + q, device(other, oa[p], ob[q]), "full")
    own_col.wait()
    own_row.wait()
    to_smem.wait()
    for n in range(128):
        row = source_smem[0, n]
        columns[BLOCK * n : BLOCK * n + BLOCK, :] = col_factor[row]
    for n in range(8):
        cols = slice(256 * n, 256 * n + 256)
        partial[:, cols] = partial[:, cols] - dot_nt(row_factor[...], columns[cols, :])
    for d in ORDER[START - 1 :]:
        update_wait(d).wait()
    for copy in sent:
        copy.wait_send()


def combine(recv_ref, row_ref, gather_ref, partial_ref, out_ref, panel_ref):
    step = pl.program_id(0)
    grid = lax.axis_index("grid")
    width = out_ref.shape[1]
    head = BLOCK * START

    @pl.when(step == 0)
    def _():
        pick = onehot(iota((64, 512), 1) == grid * 64 + iota((64, 512), 0))
        panel_ref[...] = dot_nt(pick, row_ref[...]).astype(jnp.bfloat16)

    cols = pl.ds(pl.multiple_of(step * width, 128), width)
    total = partial_ref[:, cols] + dot(gather_ref[:, head:512], recv_ref[head:512, cols])
    out_ref[...] = total.astype(jnp.bfloat16)


def local(child_update, child_panel, panel_entries, panel_inverse, block_owner, child_dest, child_rows):
    vmem = pl.BlockSpec(memory_space=pltpu.VMEM)
    bf16 = jnp.bfloat16
    dma = pltpu.SemaphoreType.DMA
    recv_update, row_factor, gather, partial = pl.pallas_call(
        exchange,
        out_shape=(
            jax.ShapeDtypeStruct((512, 2048), bf16),
            jax.ShapeDtypeStruct((1024, 512), bf16),
            jax.ShapeDtypeStruct((1024, 512), bf16),
            jax.ShapeDtypeStruct((1024, 2048), jnp.float32),
        ),
        in_specs=[pl.BlockSpec(memory_space=pltpu.HBM)] * 7,
        out_specs=(vmem, vmem, vmem, vmem),
        scratch_shapes=[
            pltpu.VMEM((256, BLOCK, 512), bf16),
            pltpu.VMEM((1, 128), jnp.int32),
            pltpu.SMEM((1, 128), jnp.int32),
            pltpu.SMEM((8, 128), jnp.int32),
            pltpu.VMEM((2048, 512), bf16),
            pltpu.VMEM((512, 2048), bf16),
            pltpu.VMEM((512, 128), bf16),
            pltpu.VMEM((512, 128), bf16),
            pltpu.VMEM((8, 64, 128), bf16),
            pltpu.VMEM((512, 128), bf16),
            pltpu.VMEM((128, 512), bf16),
            pltpu.VMEM((8, BLOCK, 512), bf16),
            dma((32,)), dma((32,)), dma((32,)), dma((32,)),
            dma((8,)), dma((8,)), dma((8,)), dma((8,)),
            dma((36,)), dma((36,)), dma((5,)), dma((7,)),
            pltpu.VMEM((8, 128), jnp.int32),
            pltpu.VMEM((4, 128), jnp.int32),
            pltpu.VMEM((16, 16), jnp.int32),
            pltpu.VMEM((64, 256), bf16),
            pltpu.VMEM((256, 2048), bf16),
            pltpu.VMEM((64, 1024), bf16),
            pltpu.VMEM((512, 512), bf16),
        ],
        compiler_params=pltpu.CompilerParams(
            collective_id=0, has_side_effects=True, vmem_limit_bytes=30 * 1024 * 1024
        ),
        name="exchange",
    )(
        *(
            pltpu.with_memory_space_constraint(operand, pltpu.HBM)
            for operand in (
                block_owner.reshape(8, 128), child_dest.reshape(4, 128), child_rows,
                child_panel, child_update, panel_entries, panel_inverse,
            )
        )
    )
    width = WIDTH
    steps = 2048 // width
    out, panel = pl.pallas_call(
        combine,
        out_shape=(jax.ShapeDtypeStruct((1024, 2048), bf16), jax.ShapeDtypeStruct((64, 1024), bf16)),
        grid=(steps,),
        in_specs=[vmem] * 4,
        out_specs=(
            pl.BlockSpec((1024, width), lambda i: (0, i)),
            pl.BlockSpec((64, 1024), lambda i: (0, 0)),
        ),
        compiler_params=pltpu.CompilerParams(
            dimension_semantics=("arbitrary",), vmem_limit_bytes=32 * 1024 * 1024
        ),
        name="combine",
    )(recv_update, row_factor, gather, partial)
    return out, panel


def solution(mesh):
    placed = (
        P("cube", "grid"),
        P("grid", "cube"),
        P("grid", "cube"),
        P(),
        P(),
        P(),
        P("cube", None),
    )
    return jax.shard_map(
        local,
        mesh=mesh,
        in_specs=placed,
        out_specs=(P("cube", "grid"), P("grid", "cube")),
        check_vma=False,
    )
```

```python
import functools

import jax
import jax.numpy as jnp
from jax import lax
from jax.experimental import pallas as pl
from jax.experimental.pallas import tpu as pltpu
from jax.sharding import PartitionSpec as P

MESH = pl.DeviceIdType.MESH
BLOCK = 16
PIECE = 128
INJECT = (0, 8, 1, 1, 1, 1, 1, 31)
NEAR_FIRST = False
DIRECT2 = (False, False, False, True)
WIDTH = 512
START = 16


def iota(shape, dim):
    return lax.broadcasted_iota(jnp.int32, shape, dim)


def onehot(cond, dtype=jnp.bfloat16):
    return jnp.where(cond, 1.0, 0.0).astype(dtype)


def dot(lhs, rhs):
    return jnp.dot(lhs, rhs, preferred_element_type=jnp.float32)


def dot_nt(lhs, rhs):
    return lax.dot_general(lhs, rhs, (((1,), (1,)), ((), ())), preferred_element_type=jnp.float32)


def hops(d):
    return min(d // 8, 4 - d // 8) + min(d // 2 % 4, 4 - d // 2 % 4)


ORDER = sorted(range(1, 32), key=hops if NEAR_FIRST else lambda d: -hops(d))
SLOT = {d: n + 1 for n, d in enumerate(ORDER)}
SLOT[0] = 0


def send_tables(cube, owner_ref, dest_ref, rows_ref):
    owners = owner_ref[...]
    hot = jnp.concatenate(
        [onehot(iota((32, 128), 0) == owners[r : r + 1, :], jnp.float32) for r in range(8)], axis=0
    )
    before = onehot(iota((128, 128), 0) < iota((128, 128), 1))
    running = dot(hot.astype(jnp.bfloat16), before)
    picked = hot * running
    rank = jnp.concatenate(
        [jnp.sum(picked[32 * r : 32 * r + 32], axis=0, keepdims=True) for r in range(8)], axis=0
    )
    owners_f = owners.astype(jnp.float32)
    slot = rank + 8.0 * iota((8, 128), 0).astype(jnp.float32)
    table = jnp.concatenate([owners_f, slot], axis=0).astype(jnp.bfloat16)
    count = jnp.sum(onehot(owners == cube, jnp.float32), axis=1, keepdims=True)
    live = onehot(count > (iota((8, 128), 1) // BLOCK).astype(jnp.float32), jnp.float32)
    dest = dest_ref[...]
    child_owner, child_slot = [], []
    for q in range(4):
        row = dest[q : q + 1, :]
        at = onehot(iota((128, 128), 0) == row % 128)
        found = dot(table, at)
        mask = onehot(iota((8, 128), 0) == row // 128, jnp.float32)
        child_owner.append(jnp.sum(found[0:8] * mask, axis=0, keepdims=True))
        child_slot.append(jnp.sum(found[8:16] * mask, axis=0, keepdims=True))
    child_owner = jnp.concatenate(child_owner + child_owner, axis=0)
    child_slot = jnp.concatenate(child_slot + child_slot, axis=0)
    expand = onehot(iota((128, 256), 0) == (cube % 8) * BLOCK + iota((128, 256), 1) // BLOCK)
    own = dot(child_owner.astype(jnp.bfloat16), expand)
    own = jnp.sum(jnp.where(iota((8, 256), 0) == cube // 8, own, 0.0), axis=0, keepdims=True)
    spread = onehot(iota((16, 256), 1) % BLOCK == iota((16, 256), 0))
    rows = dot(rows_ref[...].astype(jnp.float32).astype(jnp.bfloat16), spread)
    rows = jnp.sum(jnp.where(iota((16, 256), 1) // BLOCK == iota((16, 256), 0), rows, 0.0), axis=0, keepdims=True)
    send = (own * BLOCK + rows).astype(jnp.int32)
    return send, live, child_owner, child_slot


def receive_table(cube, origins, child_owner, child_slot):
    mine = jnp.where(child_owner == cube.astype(jnp.float32), child_slot + 1.0, 0.0).astype(jnp.bfloat16)
    places = []
    for q in range(4):
        lane = iota((1, 128), 1) // BLOCK
        wanted = jnp.zeros((1, 128), jnp.int32)
        for n in range(8):
            wanted = jnp.where(lane == n, origins[8 * q + n], wanted)
        joined = jnp.zeros((8, 128), jnp.float32)
        for p in range(4):
            pick = onehot(iota((128, 128), 0) // BLOCK + 8 * p == wanted)
            part = dot(mine, pick)
            joined = joined + jnp.where(iota((8, 128), 0) == p, part, 0.0)
        joined = jnp.sum(joined, axis=0, keepdims=True)
        within = (iota((1, 128), 1) % BLOCK).astype(jnp.float32)
        places.append(jnp.where(joined > 0.5, (joined - 1.0) * BLOCK + within, -1.0).astype(jnp.int32))
    return places


def exchange(
    owner_hbm,
    dest_hbm,
    rows_hbm,
    panel_hbm,
    update_hbm,
    entries_hbm,
    inverse_hbm,
    recv_update,
    row_factor,
    gather_ref,
    partial,
    col_factor,
    source_ref,
    source_smem,
    owner_smem,
    columns,
    send_update,
    send_panel,
    recv_panel,
    z_send,
    z_recv,
    piece,
    blocks,
    up_send,
    up_recv,
    pan_send,
    pan_recv,
    za_send,
    za_recv,
    zg_send,
    zg_recv,
    ag_send,
    ag_recv,
    local_sem,
    load_sem,
    owner_ref,
    dest_ref,
    rows_ref,
    panel_ref,
    update_ref,
    entries_ref,
    inverse_ref,
):
    sources = (owner_hbm, dest_hbm, rows_hbm, panel_hbm, update_hbm, entries_hbm, inverse_hbm)
    targets = (owner_ref, dest_ref, rows_ref, panel_ref, update_ref, entries_ref, inverse_ref)
    loads = [
        pltpu.make_async_copy(source, target, load_sem.at[n])
        for n, (source, target) in enumerate(zip(sources, targets))
    ]
    for load in loads:
        load.start()
    to_owners = pltpu.make_async_copy(owner_hbm, owner_smem, local_sem.at[4])
    to_owners.start()
    cube = lax.axis_index("cube")
    grid = lax.axis_index("grid")
    core, x, y = cube % 2, (cube // 2) % 4, cube // 8

    ys = [8 * ((y + k) % 4) for k in range(4)]
    xs = [2 * ((x + k) % 4) for k in range(4)]
    cores = [core, 1 - core]

    def peer(d):
        return ys[d // 8] + xs[d // 2 % 4] + cores[d % 2]

    def origin(d):
        return ys[-(d // 8) % 4] + xs[-(d // 2 % 4) % 4] + cores[d % 2]

    barrier = pltpu.get_barrier_semaphore()

    for d in sorted(range(1, 32), key=hops, reverse=True):
        pl.semaphore_signal(barrier, inc=1, device_id={"cube": peer(d)}, device_id_type=MESH)
    for d in (4, 3, 5, 2, 6, 1, 7):
        pl.semaphore_signal(barrier, inc=1, device_id={"grid": (grid + d) % 8}, device_id_type=MESH)

    for load in loads[:3]:
        load.wait()
    send, live, child_owner, child_slot = send_tables(cube, owner_ref, dest_ref, rows_ref)
    route = onehot(iota((512, 256), 0) == send)
    loads[3].wait()
    panel_in = jnp.concatenate([panel_ref[...], jnp.zeros((64, 256), jnp.bfloat16)], axis=0)
    send_panel[...] = dot_nt(route, panel_in).astype(jnp.bfloat16)

    def rows16(owner):
        return pl.ds(pl.multiple_of(owner * BLOCK, BLOCK), BLOCK)

    def slot16(d):
        return pl.ds(BLOCK * SLOT[d], BLOCK)

    pl.semaphore_wait(barrier, 38)

    def panel_copy(d):
        to = peer(d)
        return pltpu.make_async_remote_copy(
            send_panel.at[rows16(to), :], recv_panel.at[slot16(d), :],
            pan_send.at[d], pan_recv.at[d], device_id={"cube": to}, device_id_type=MESH,
        )

    def panel_wait(d):
        return pltpu.make_async_remote_copy(
            send_panel.at[rows16(peer(d)), :], recv_panel.at[slot16(d), :],
            pan_send.at[d], pan_recv.at[d], device_id={"cube": peer(d)}, device_id_type=MESH,
        )

    def update_copy(d):
        to = peer(d)
        return pltpu.make_async_remote_copy(
            send_update.at[rows16(to), :], recv_update.at[slot16(d), :],
            up_send.at[d], up_recv.at[d], device_id={"cube": to}, device_id_type=MESH,
        )

    def update_wait(d):
        return pltpu.make_async_remote_copy(
            send_update.at[rows16(peer(d)), :], recv_update.at[slot16(d), :],
            up_send.at[d], up_recv.at[d], device_id={"cube": peer(d)}, device_id_type=MESH,
        )

    far_first = sorted(range(1, 32), key=hops, reverse=True)
    for d in far_first:
        panel_copy(d).start()
    loads[4].wait()
    for n in range(4):
        cols = slice(512 * n, 512 * n + 512)
        send_update[:, cols] = dot(route, update_ref[:, cols]).astype(jnp.bfloat16)
    by_slot = {n: d for d, n in SLOT.items()}
    places = receive_table(cube, [origin(by_slot[n]) for n in range(32)], child_owner, child_slot)
    pending = list(ORDER)
    stage = iter(INJECT)

    def inject():
        count = next(stage)
        for d in pending[:count]:
            update_copy(d).start()
        del pending[:count]

    inject()
    own_update = pltpu.make_async_copy(
        send_update.at[rows16(cube), :], recv_update.at[slot16(0), :], local_sem.at[0]
    )
    own_update.start()
    recv_panel[slot16(0), :] = send_panel[rows16(cube), :]
    for r in range(8):
        gather = jnp.concatenate(
            [onehot(iota((128, 128), 0) + r * 128 == places[q]) for q in range(4)], axis=1
        )
        gather_ref[128 * r : 128 * r + 128, :] = gather
    for d in far_first:
        panel_wait(d).wait()
    inject()

    loads[5].wait()
    loads[6].wait()
    panel_t = recv_panel[...].astype(jnp.float32).T.astype(jnp.bfloat16)
    for r in range(8):
        total = dot_nt(panel_t, gather_ref[128 * r : 128 * r + 128, :])[0:64]
        entries = entries_ref[:, 128 * r : 128 * r + 128].astype(jnp.float32)
        total = total + jnp.where(live[r : r + 1, :] > 0.5, entries, 0.0)
        z_send[r] = total.astype(jnp.bfloat16)

    def zrows(g):
        return pl.ds(pl.multiple_of(g * 64, 64), 64)

    def z_copy(d, into):
        to = (grid + d) % 8
        return pltpu.make_async_remote_copy(
            z_send.at[to], z_recv.at[zrows(into), :],
            za_send.at[d], za_recv.at[d], device_id={"grid": to}, device_id_type=MESH,
        )

    for d in (4, 3, 5, 2, 6, 1, 7):
        z_copy(d, grid).start()
    z_recv[zrows(grid), :] = z_send[grid]
    for d in (4, 3, 5, 2, 6, 1, 7):
        z_copy(d, (grid + 8 - d) % 8).wait()
    front = z_recv[...].astype(jnp.float32).T.astype(jnp.bfloat16)
    own_factor = dot(front, inverse_ref[...]).astype(jnp.bfloat16)
    piece[...] = own_factor
    blocks[...] = own_factor.reshape(8, BLOCK, 512)

    a = x + core * (y - x)
    b = y + core * (x - y)

    def device(k, p, q):
        return ((q + k * (p - q)) * 4 + p + k * (q - p)) * 2 + k

    def stretch(owner, low, size):
        return pl.ds(pl.multiple_of(owner * PIECE + low, 64), size)

    parts = {"full": (0, 128), "top": (0, 64), "bottom": (64, 64)}

    def ag_copy(m, owner, part, to):
        low, size = parts[part]
        there = col_factor.at[pl.ds(owner * 8 + low // BLOCK, size // BLOCK)]
        return pltpu.make_async_remote_copy(
            there, there, ag_send.at[m], ag_recv.at[m], device_id={"cube": to}, device_id_type=MESH
        )

    def ag_own(m, to):
        return pltpu.make_async_remote_copy(
            blocks, col_factor.at[pl.ds(cube * 8, 8)],
            ag_send.at[m], ag_recv.at[m], device_id={"cube": to}, device_id_type=MESH,
        )

    off = (0, 3, 1, 2)
    pa = [(a + o) % 4 for o in off]
    pb = [(b + o) % 4 for o in off]
    a_next, a_prev = device(core, pa[2], b), device(core, pa[1], b)
    b_next, b_prev = device(core, a, pb[2]), device(core, a, pb[1])
    b_far = device(core, a, pb[3])
    sibling = cube + 1 - 2 * core
    sent = []

    def go(copy):
        copy.start()
        sent.append(copy)

    def got(m, owner, part):
        ag_copy(m, owner, part, a_next).wait_recv()

    def to_sibling(p, q):
        go(ag_copy(20 + 4 * p + q, device(core, pa[p], pb[q]), "full", sibling))

    def phase2(p):
        go(ag_copy(4 + 4 * p, device(core, pa[p], b), "full", b_next))
        go(ag_copy(5 + 4 * p, device(core, pa[p], b), "full", b_prev))
        if DIRECT2[p]:
            go(ag_copy(6 + 4 * p, device(core, pa[p], b), "full", b_far))
        to_sibling(p, 0)

    def near(p):
        below, above = device(core, pa[p], pb[1]), device(core, pa[p], pb[2])
        got(4 + 4 * p, below, "full")
        if not DIRECT2[p]:
            go(ag_copy(6 + 4 * p, below, "top", b_next))
        to_sibling(p, 1)
        got(5 + 4 * p, above, "full")
        if not DIRECT2[p]:
            go(ag_copy(7 + 4 * p, above, "bottom", b_prev))
        to_sibling(p, 2)

    def far(p):
        owner = device(core, pa[p], pb[3])
        if DIRECT2[p]:
            got(6 + 4 * p, owner, "full")
        else:
            got(6 + 4 * p, owner, "top")
            got(7 + 4 * p, owner, "bottom")
        to_sibling(p, 3)

    def z_part(m, owner, part, to):
        low, size = parts[part]
        there = row_factor.at[stretch(owner, low, size), :]
        return pltpu.make_async_remote_copy(
            there, there, zg_send.at[m], zg_recv.at[m], device_id={"grid": to}, device_id_type=MESH
        )

    def z_own(m, to):
        return pltpu.make_async_remote_copy(
            piece, row_factor.at[stretch(grid, 0, 128), :],
            zg_send.at[m], zg_recv.at[m], device_id={"grid": to}, device_id_type=MESH,
        )

    def gz(o):
        return (grid + 8 + o) % 8

    def z_got(m, owner, part):
        z_part(m, owner, part, gz(1)).wait_recv()

    def z_relay():
        z_got(2, gz(-2), "full")
        go(z_part(4, gz(-2), "full", gz(1)))
        go(z_part(6, gz(-2), "top", gz(2)))
        z_got(3, gz(2), "full")
        go(z_part(5, gz(2), "full", gz(-1)))
        go(z_part(7, gz(2), "bottom", gz(-2)))

    go(ag_own(0, a_next))
    go(ag_own(1, a_prev))
    go(ag_own(2, device(core, pa[3], b)))
    go(z_own(2, gz(2)))
    go(z_own(3, gz(-2)))
    go(z_own(0, gz(1)))
    go(z_own(1, gz(-1)))
    go(ag_own(4, b_next))
    go(ag_own(5, b_prev))
    if DIRECT2[0]:
        go(ag_own(6, b_far))
    go(ag_own(20, sibling))
    own_col = pltpu.make_async_copy(blocks, col_factor.at[pl.ds(cube * 8, 8)], local_sem.at[1])
    own_row = pltpu.make_async_copy(piece, row_factor.at[stretch(grid, 0, 128), :], local_sem.at[2])
    own_col.start()
    own_row.start()
    inject()

    left, right, across = device(core, pa[1], b), device(core, pa[2], b), device(core, pa[3], b)
    to_owners.wait()
    range_owner = owner_ref[pl.ds(grid, 1), :]
    range_rank = jnp.zeros((1, 128), jnp.int32)
    for n in range(127):
        earlier = (range_owner == owner_smem[grid, n]) & (iota((1, 128), 1) > n)
        range_rank = range_rank + jnp.where(earlier, 1, 0)
    source_ref[...] = range_owner * 8 + range_rank
    got(0, left, "full")
    phase2(1)
    inject()
    got(1, right, "full")
    phase2(2)
    inject()
    near(0)
    got(2, across, "full")
    phase2(3)
    inject()
    to_smem = pltpu.make_async_copy(source_ref, source_smem, local_sem.at[3])
    to_smem.start()
    z_relay()
    near(1)
    inject()
    near(2)
    far(0)
    near(3)
    inject()
    assert not pending
    far(1)
    far(2)
    far(3)
    for d in ORDER[: START - 1]:
        update_wait(d).wait()
    own_update.wait()
    head = BLOCK * START
    for n in range(8):
        cols = slice(256 * n, 256 * n + 256)
        partial[:, cols] = dot(gather_ref[:, 0:head], recv_update[0:head, cols])
    z_got(0, gz(-1), "full")
    z_got(1, gz(1), "full")
    z_got(4, gz(-3), "full")
    z_got(5, gz(3), "full")
    z_got(6, gz(4), "top")
    z_got(7, gz(4), "bottom")
    other = 1 - core
    oa = [(b + o) % 4 for o in off]
    ob = [(a + o) % 4 for o in off]
    for p in range(4):
        for q in range(4):
            got(20 + 4 * p + q, device(other, oa[p], ob[q]), "full")
    own_col.wait()
    own_row.wait()
    to_smem.wait()
    for n in range(128):
        row = source_smem[0, n]
        columns[BLOCK * n : BLOCK * n + BLOCK, :] = col_factor[row]
    for n in range(8):
        cols = slice(256 * n, 256 * n + 256)
        partial[:, cols] = partial[:, cols] - dot_nt(row_factor[...], columns[cols, :])
    for d in ORDER[START - 1 :]:
        update_wait(d).wait()
    for copy in sent:
        copy.wait_send()


def combine(recv_ref, row_ref, gather_ref, partial_ref, out_ref, panel_ref):
    step = pl.program_id(0)
    grid = lax.axis_index("grid")
    width = out_ref.shape[1]
    head = BLOCK * START

    @pl.when(step == 0)
    def _():
        pick = onehot(iota((64, 512), 1) == grid * 64 + iota((64, 512), 0))
        panel_ref[...] = dot_nt(pick, row_ref[...]).astype(jnp.bfloat16)

    cols = pl.ds(pl.multiple_of(step * width, 128), width)
    total = partial_ref[:, cols] + dot(gather_ref[:, head:512], recv_ref[head:512, cols])
    out_ref[...] = total.astype(jnp.bfloat16)


def local(child_update, child_panel, panel_entries, panel_inverse, block_owner, child_dest, child_rows):
    vmem = pl.BlockSpec(memory_space=pltpu.VMEM)
    bf16 = jnp.bfloat16
    dma = pltpu.SemaphoreType.DMA
    recv_update, row_factor, gather, partial = pl.pallas_call(
        exchange,
        out_shape=(
            jax.ShapeDtypeStruct((512, 2048), bf16),
            jax.ShapeDtypeStruct((1024, 512), bf16),
            jax.ShapeDtypeStruct((1024, 512), bf16),
            jax.ShapeDtypeStruct((1024, 2048), jnp.float32),
        ),
        in_specs=[pl.BlockSpec(memory_space=pltpu.HBM)] * 7,
        out_specs=(vmem, vmem, vmem, vmem),
        scratch_shapes=[
            pltpu.VMEM((256, BLOCK, 512), bf16),
            pltpu.VMEM((1, 128), jnp.int32),
            pltpu.SMEM((1, 128), jnp.int32),
            pltpu.SMEM((8, 128), jnp.int32),
            pltpu.VMEM((2048, 512), bf16),
            pltpu.VMEM((512, 2048), bf16),
            pltpu.VMEM((512, 128), bf16),
            pltpu.VMEM((512, 128), bf16),
            pltpu.VMEM((8, 64, 128), bf16),
            pltpu.VMEM((512, 128), bf16),
            pltpu.VMEM((128, 512), bf16),
            pltpu.VMEM((8, BLOCK, 512), bf16),
            dma((32,)), dma((32,)), dma((32,)), dma((32,)),
            dma((8,)), dma((8,)), dma((8,)), dma((8,)),
            dma((36,)), dma((36,)), dma((5,)), dma((7,)),
            pltpu.VMEM((8, 128), jnp.int32),
            pltpu.VMEM((4, 128), jnp.int32),
            pltpu.VMEM((16, 16), jnp.int32),
            pltpu.VMEM((64, 256), bf16),
            pltpu.VMEM((256, 2048), bf16),
            pltpu.VMEM((64, 1024), bf16),
            pltpu.VMEM((512, 512), bf16),
        ],
        compiler_params=pltpu.CompilerParams(
            collective_id=0, has_side_effects=True, vmem_limit_bytes=30 * 1024 * 1024
        ),
        name="exchange",
    )(
        *(
            pltpu.with_memory_space_constraint(operand, pltpu.HBM)
            for operand in (
                block_owner.reshape(8, 128), child_dest.reshape(4, 128), child_rows,
                child_panel, child_update, panel_entries, panel_inverse,
            )
        )
    )
    width = WIDTH
    steps = 2048 // width
    out, panel = pl.pallas_call(
        combine,
        out_shape=(jax.ShapeDtypeStruct((1024, 2048), bf16), jax.ShapeDtypeStruct((64, 1024), bf16)),
        grid=(steps,),
        in_specs=[vmem] * 4,
        out_specs=(
            pl.BlockSpec((1024, width), lambda i: (0, i)),
            pl.BlockSpec((64, 1024), lambda i: (0, 0)),
        ),
        compiler_params=pltpu.CompilerParams(
            dimension_semantics=("arbitrary",), vmem_limit_bytes=32 * 1024 * 1024
        ),
        name="combine",
    )(recv_update, row_factor, gather, partial)
    return out, panel


def solution(mesh):
    placed = (
        P("cube", "grid"),
        P("grid", "cube"),
        P("grid", "cube"),
        P(),
        P(),
        P(),
        P("cube", None),
    )
    return jax.shard_map(
        local,
        mesh=mesh,
        in_specs=placed,
        out_specs=(P("cube", "grid"), P("grid", "cube")),
        check_vma=False,
    )
```
